512 devices in a mesh: rows: 32 (over z, core), mem: 16 (over y, x).
Axes of the slice: x: 4, y: 4, z: 16, core: 2. Of those that a mesh axis runs over, the one named last changes fastest.
Arguments:
- ensemble_state: float32 [16384, 4096], P('rows', 'mem'), may hold values from -6 to 6
- predicted: float32 [12288, 4096], P('rows', 'mem'), may hold values from -6 to 6
- perturbed: float32 [12288, 4096], P('rows', 'mem'), may hold values from -9 to 9
- obs_variance: float32 [3, 256], replicated, may hold values from 0.25 to 4
- owners: int32 [3], replicated, may hold values from 0 to 31, as said below
- positions: int32 [3, 256], replicated, may hold values from 0 to 383, as said below
Outputs:
- analysis_state: float32 [16384, 4096], P('rows', 'mem')
- analysis_obs: float32 [12288, 4096], P('rows', 'mem')
The draws below stay inside these ranges and needn't reach their ends.
Inputs may be any that keep to these rules, and one draw needn't show every extreme that they name: The 3 owners are distinct; the first and the last index of rows are always among them. Each batch's 256 positions are distinct; every batch holds position 0 and position 383.
All inputs are finite; a program needn't handle non-finite values.
Results may differ from the reference program's by a relative error of at most 0.0003.
Values sent between devices are 32-bit elements; how exact they have to be, the bound alone decides.
No kernel may reach another device: no remote copies, remote signals or barrier semaphores. Data moves between devices by JAX's collectives and lax.ppermute only.
A program may use at most 64 MiB of HBM per device.

```python
import math
import jax
import jax.numpy as jnp
import numpy as np
from jax import lax

MEMBERS = 4096
P_SIZE = 256
BATCHES = 3
SROW_DEV = 512
OBS_DEV = 384
S = 16384
OROWS = 12288


def draw_owners(key, part):
    total = S // SROW_DEV
    first_key = jax.random.fold_in(key, 11)
    second_key = jax.random.fold_in(key, 12)
    middle = jax.random.permutation(first_key, total - 2)[:BATCHES - 2].astype(jnp.int32) + 1
    chosen = jnp.concatenate([jnp.array([0, total - 1], jnp.int32), middle])
    order = jax.random.permutation(second_key, BATCHES).astype(jnp.int32)
    return jnp.take(chosen, order, axis=0).astype(jnp.int32)


def one_batch(key):
    first_key = jax.random.fold_in(key, 21)
    second_key = jax.random.fold_in(key, 22)
    middle = jax.random.permutation(first_key, OBS_DEV - 2)[:P_SIZE - 2].astype(jnp.int32) + 1
    chosen = jnp.concatenate([jnp.array([0, OBS_DEV - 1], jnp.int32), middle])
    order = jax.random.permutation(second_key, P_SIZE).astype(jnp.int32)
    return jnp.take(chosen, order, axis=0).astype(jnp.int32)


def draw_positions(key, part):
    base_key = jax.random.fold_in(key, 31)
    key_list = jax.random.split(base_key, BATCHES)
    return jax.vmap(one_batch)(key_list).astype(jnp.int32)


def draw_predicted(key, part):
    first_key = jax.random.fold_in(key, 41)
    tap_table = np.floor(64.0 * 0.93 ** np.arange(48) + 0.5) / 64.0
    tap_count = 48
    noise_grid = jax.random.randint(first_key, (OROWS + tap_count - 1, MEMBERS), -512, 512).astype(jnp.float32) / 128.0
    noise_variance = (1024.0 * 1024.0 - 1.0) / 12.0 / 16384.0
    spread_factor = 1.0
    summed = jnp.zeros((OROWS, MEMBERS), jnp.float32)
    for step_lag in range(tap_count):
        summed = summed + float(tap_table[step_lag]) * noise_grid[step_lag:step_lag + OROWS]
    scaling = spread_factor / math.sqrt(noise_variance * float(np.sum(tap_table * tap_table)))
    return jnp.clip(summed * scaling, -6.0, 6.0).astype(jnp.float32)


def levels(stream_key, shape, cuts, least, high):
    gain = 1.0
    for axis_at, parts in cuts:
        draws = jax.random.uniform(jax.random.fold_in(jax.random.fold_in(stream_key, 6), axis_at), (parts,), jnp.float32, least / len(cuts), high / len(cuts))
        gain = gain * jnp.repeat(jnp.exp(draws), shape[axis_at] // parts).reshape((-1,) + (1,) * (len(shape) - 1 - axis_at))
    return gain


def centred(key, dims, width, reach, pieces=(), dtype=jnp.bfloat16):
    entries = jax.random.normal(key, dims, jnp.float32) * width
    if len(pieces) > 0:
        entries = levels(key, dims, pieces, -0.22, 0.18) * entries
    return jnp.clip(entries, min=-reach, max=reach).astype(dtype)


def setup_inputs(seed: int = 0) -> dict:
    streams_of = jax.random.split(jax.random.key(seed), 7)
    ensemble_state = centred(streams_of[0], (S, MEMBERS), 1.0, 6.0, ((0, 32), (1, 16)), jnp.float32)
    predicted = draw_predicted(jax.random.fold_in(streams_of[6], 71), 0)
    perturbed = centred(streams_of[2], (OROWS, MEMBERS), 1.5, 9.0, ((0, 32), (1, 16)), jnp.float32)
    obs_variance = jnp.clip(jnp.exp(jax.random.uniform(streams_of[3], (BATCHES, P_SIZE), jnp.float32, math.log(0.25), math.log(4.0))), 0.25, 4.0)
    owners = draw_owners(jax.random.fold_in(streams_of[6], 71), 0)
    positions = draw_positions(jax.random.fold_in(streams_of[6], 71), 0)
    return dict(ensemble_state=ensemble_state, predicted=predicted, perturbed=perturbed, obs_variance=obs_variance, owners=owners, positions=positions)


exact = lax.Precision.HIGHEST

def reference(ensemble_state, predicted, perturbed, obs_variance, owners, positions):
    state_now = ensemble_state
    obs_now = predicted
    for number in range(BATCHES):
        row_ids = (owners[number] * OBS_DEV + positions[number]).astype(jnp.int32)
        observed = jnp.take(obs_now, row_ids, axis=0)
        innovation = jnp.take(perturbed, row_ids, axis=0) - observed
        anomaly = observed - jnp.sum(observed, axis=1, keepdims=True) / MEMBERS
        cross_state = jnp.einsum('rm,pm->rp', state_now, anomaly, precision=exact) / (MEMBERS - 1)
        cross_obs = jnp.einsum('rm,pm->rp', obs_now, anomaly, precision=exact) / (MEMBERS - 1)
        inner_cov = jnp.einsum('qm,pm->qp', anomaly, anomaly, precision=exact) / (MEMBERS - 1)
        inner_cov = inner_cov + jnp.diag(obs_variance[number])
        factor = jnp.linalg.cholesky(inner_cov)
        weights = jax.scipy.linalg.cho_solve((factor, True), innovation)
        state_now = state_now + jnp.dot(cross_state, weights, precision=exact)
        obs_now = obs_now + jnp.dot(cross_obs, weights, precision=exact)
    return (state_now, obs_now)
```

```python
import jax
import jax.numpy as jnp
from jax import lax
from jax.sharding import PartitionSpec as P

BATCHES = 3
exact = lax.Precision.HIGHEST
HALF_A = ((0, 0), (1, 0), (2, 0), (1, 1), (2, 1), (2, 2))
HALF_B = ((3, 1), (3, 2), (3, 3), (4, 2), (4, 3), (4, 4))


def mm(a, b):
    return lax.dot_general(a, b, (((1,), (0,)), ((), ())), precision=exact)


def mm_nt(a, b):
    return lax.dot_general(a, b, (((1,), (1,)), ((), ())), precision=exact)


def mm_tn(a, b):
    return lax.dot_general(a, b, (((0,), (0,)), ((), ())), precision=exact)


def inverse(cov):
    factor = jnp.linalg.cholesky(cov)
    low = lax.linalg.triangular_solve(factor, jnp.eye(cov.shape[0], dtype=cov.dtype), left_side=True, lower=True)
    return mm_tn(low, low)


def chain(g, r, e):
    inv0 = inverse(g[0, 0] + jnp.diag(r[0]))
    k10 = mm(g[1, 0], inv0)
    k20 = mm(g[2, 0], inv0)
    half = 0.5 * g[3, 3]
    t1 = g[3, 1].T + mm(k10, half)
    t2 = g[3, 2].T + mm(k20, half)
    te = g[4, 3] - mm(k10, half)
    z11 = mm_nt(k10, t1)
    s11 = g[1, 1] + z11 + z11.T
    c21 = g[2, 1] + mm_nt(k20, t1) + mm_nt(t2, k10)
    z22 = mm_nt(k20, t2)
    c22 = g[2, 2] + z22 + z22.T
    ce2 = g[4, 2] - mm_nt(k10, t2) + mm_nt(te, k20)
    ze = mm_nt(k10, te)
    cee = g[4, 4] - ze - ze.T
    inv1 = inverse(s11 + jnp.diag(r[1]))
    k21 = mm(c21, inv1)
    t22 = ce2.T + mm(k21, 0.5 * cee)
    z = mm_nt(k21, t22)
    inv2 = inverse(c22 + z + z.T + jnp.diag(r[2]))
    e0 = e[0]
    e1 = e[1] - mm(k10, e0)
    e2 = e[2] - mm(k20, e0) - mm(k21, e1)
    w2 = mm(inv2, e2)
    w1 = mm(inv1, e1 + mm(ce2 + mm_nt(cee, k21), w2))
    k21w2 = mm_tn(k21, w2)
    v3 = mm_tn(k10, w1 - k21w2) + mm_tn(k20, w2)
    w0 = mm(inv0, e0 + mm(g[3, 1], w1) + mm(g[3, 2], w2) + mm(g[3, 3], v3) + mm_tn(g[4, 3], k21w2))
    return jnp.concatenate([w0, w1, w2, v3, k21w2], axis=0)


def make(n_rows, n_mem):
    cores = 2
    n_z = n_rows // cores
    same_core = [[z * cores + c for z in range(n_z)] for c in range(cores)]
    swap = [(i, i ^ 1) for i in range(n_rows)]

    def on_device(state, predicted, perturbed, obs_variance, owners, positions):
        p = positions.shape[1]
        local = state.shape[1]
        members = local * n_mem
        part = p // n_rows
        row = lax.axis_index("rows")
        core = row % cores

        mine = jnp.argmax(owners == row)
        picked = positions[mine]
        out = jnp.concatenate(
            [
                jnp.take(predicted, picked, axis=0).reshape(n_rows, part, local),
                jnp.take(perturbed, picked, axis=0).reshape(n_rows, part, local),
            ],
            axis=1,
        )
        got = lax.all_to_all(out, "rows", 0, 0, tiled=True)
        piece = jnp.take(got, owners, axis=0)
        here = lax.all_gather(piece, "rows", axis_index_groups=same_core)
        there = lax.ppermute(here, "rows", swap)
        even = jnp.where(core == 0, here, there)
        odd = jnp.where(core == 0, there, here)
        both = jnp.stack([even, odd], axis=1).reshape(n_rows, BATCHES, 2, part, local)
        both = both.transpose(1, 2, 0, 3, 4).reshape(BATCHES, 2, p, local)
        obs = both[:, 0]
        inno = both[:, 1] - obs

        y = jnp.concatenate([obs.reshape(3 * p, local), inno[:2].reshape(2 * p, local)], axis=0)
        mu = jnp.sum(y, axis=1) / local
        yc = y - mu[:, None]
        cross = jnp.concatenate([mm_nt(state, yc), mm_nt(predicted, yc)], axis=0)
        cross, yc = lax.optimization_barrier((cross, yc))
        cross = lax.psum(cross, "mem")
        sums = jnp.concatenate([jnp.sum(state, axis=1), jnp.sum(predicted, axis=1)])
        n_state = sums.shape[0]

        blocks = yc.reshape(5, p, local)
        half_a = jnp.concatenate([mm_nt(blocks[i], blocks[j]) for i, j in HALF_A], axis=0)
        half_b = jnp.concatenate([mm_nt(blocks[i], blocks[j]) for i, j in HALF_B], axis=0)
        gram = jnp.where(core == 0, half_a, half_b).reshape(n_mem, -1, p)
        n_gram = gram.shape[1]
        extra = jnp.concatenate([mu, sums])
        n_extra = -(-extra.shape[0] // (8 * p)) * 8
        extra = jnp.pad(extra, (0, n_extra * p - extra.shape[0])).reshape(1, n_extra, p)
        extra = jnp.broadcast_to(extra, (n_mem, n_extra, p))
        got = lax.all_to_all(jnp.concatenate([gram, extra], axis=1), "mem", 0, 0, tiled=True)
        summed = jnp.sum(got[:, :n_gram], axis=0)
        extra = got[:, n_gram:].reshape(n_mem, n_extra * p)
        mu_all = extra[:, : 5 * p]
        sums_all = extra[:, 5 * p : 5 * p + n_state]
        here = lax.all_to_all(
            jnp.broadcast_to(summed[None], (n_mem, n_gram, p)), "mem", 0, 0, tiled=True
        ).reshape(6 * p, p)
        there = lax.ppermute(here, "rows", swap)
        half_a = jnp.where(core == 0, here, there).reshape(6, p, p)
        half_b = jnp.where(core == 0, there, here).reshape(6, p, p)
        dev = mu_all - jnp.sum(mu_all, axis=0, keepdims=True) / n_mem
        scale = 1.0 / (members - 1)
        g = {}
        for half, pairs in ((half_a, HALF_A), (half_b, HALF_B)):
            for n, (i, j) in enumerate(pairs):
                between = mm_tn(dev[:, i * p : (i + 1) * p], dev[:, j * p : (j + 1) * p])
                g[i, j] = (half[n] + local * between) * scale
        v = chain(g, obs_variance, inno) * scale
        between = mm(dev, v)
        n_x = state.shape[0]
        new_state = state + mm(cross[:n_x], v) + mm_tn(sums_all[:, :n_x], between)
        new_obs = predicted + mm(cross[n_x:], v) + mm_tn(sums_all[:, n_x:], between)
        return new_state, new_obs

    return on_device


def solution(mesh):
    in_specs = (P("rows", "mem"), P("rows", "mem"), P("rows", "mem"), P(), P(), P())
    out_specs = (P("rows", "mem"), P("rows", "mem"))
    inner = make(mesh.shape["rows"], mesh.shape["mem"])

    return jax.shard_map(
        inner,
        mesh=mesh,
        in_specs=in_specs,
        out_specs=out_specs,
        check_vma=False,
    )
```

```python
import functools

import jax
import jax.numpy as jnp
from jax import lax
from jax.experimental import pallas as pl
from jax.experimental.pallas import tpu as pltpu
from jax.sharding import PartitionSpec as P

exact = lax.Precision.HIGHEST
HALF_A = ((0, 0), (1, 0), (2, 0), (1, 1), (2, 1), (2, 2))
HALF_B = ((1, 3), (2, 3), (3, 3), (2, 4), (3, 4), (4, 4))


def mm(a, b):
    return lax.dot_general(a, b, (((1,), (0,)), ((), ())), precision=exact, preferred_element_type=jnp.float32)


def mm_nt(a, b):
    return lax.dot_general(a, b, (((1,), (1,)), ((), ())), precision=exact, preferred_element_type=jnp.float32)


def mm_tn(a, b):
    return lax.dot_general(a, b, (((0,), (0,)), ((), ())), precision=exact, preferred_element_type=jnp.float32)


TILE = 8
LANES = 128


def split3(x):
    hi = x.astype(jnp.bfloat16)
    rest = x - hi.astype(jnp.float32)
    mid = rest.astype(jnp.bfloat16)
    low = (rest - mid.astype(jnp.float32)).astype(jnp.bfloat16)
    return hi, mid, low


def tn_narrow(a, b):
    ah, am, al = split3(a)
    bh, bm, bl = split3(b)
    left = jnp.concatenate([ah, ah, am, ah, am, al], axis=0)
    right = jnp.concatenate([bh, bm, bh, bl, bm, bh], axis=0)
    return lax.dot_general(left, right, (((0,), (0,)), ((), ())), preferred_element_type=jnp.float32)


def sweep_tiles(w, width):
    lane = lax.broadcasted_iota(jnp.int32, (TILE, LANES), 1)
    sub = lax.broadcasted_iota(jnp.int32, (TILE, LANES), 0)
    full = (TILE, LANES)
    n = width // TILE
    for s in range(n):
        off = s * TILE
        own = (lane >= off) & (lane < off + TILE)
        eye = jnp.where(lane - off == sub, 1.0, 0.0).astype(jnp.float32)
        cols = [[jnp.broadcast_to(w[t][0][:, off + j : off + j + 1], full) for j in range(TILE)] for t in range(n)]
        c = {}
        for j in range(TILE):
            for i in range(j, TILE):
                c[i, j] = jnp.broadcast_to(cols[s][j][i : i + 1, :], full)
        get = lambda i, j: c[max(i, j), min(i, j)]
        for j in range(TILE):
            r = 1.0 / c[j, j]
            old = {i: get(i, j) for i in range(TILE) if i != j}
            scaled = {i: old[i] * r for i in old}
            for k in range(TILE):
                for i in range(k, TILE):
                    if i != j and k != j:
                        c[i, k] = c[i, k] - scaled[i] * old[k]
            for i in old:
                c[max(i, j), min(i, j)] = scaled[i]
            c[j, j] = -r
        tcol = []
        for j in range(TILE):
            col = get(0, j)
            for i in range(1, TILE):
                col = jnp.where(sub == i, get(i, j), col)
            tcol.append(-col)
        rows, alt = [], []
        for h in range(len(w[0])):
            bz = jnp.where(own, eye, w[s][h]) if h == 0 else w[s][h]
            acc = tcol[0] * jnp.broadcast_to(bz[0:1, :], full)
            for j in range(1, TILE):
                acc = acc + tcol[j] * jnp.broadcast_to(bz[j : j + 1, :], full)
            rows.append(jnp.where(own, -acc, acc) if h == 0 else acc)
            alt.append(jnp.where(own, eye - acc, acc) if h == 0 else acc)
        spread = [[jnp.broadcast_to(a[j : j + 1, :], full) for j in range(TILE)] for a in alt]
        for t in range(n):
            if t == s:
                w[t] = rows
                continue
            new = []
            for h in range(len(alt)):
                acc = cols[t][0] * spread[h][0]
                for j in range(1, TILE):
                    acc = acc + cols[t][j] * spread[h][j]
                new.append(w[t][h] - acc)
            w[t] = new
    return w


def invert_in_place(a_ref, width=32):
    n = a_ref.shape[0]
    lane = lax.broadcasted_iota(jnp.int32, (width, n), 1)
    sub = lax.broadcasted_iota(jnp.int32, (width, n), 0)

    def step(b, _):
        base = pl.multiple_of(b * width, width)
        panel = a_ref[pl.ds(base, width), :]
        rolled = pltpu.roll(panel, lax.rem(n - base, n), 1)
        w = [
            [rolled[t * TILE : (t + 1) * TILE, h * LANES : (h + 1) * LANES] for h in range(n // LANES)]
            for t in range(width // TILE)
        ]
        w = sweep_tiles(w, width)
        w = jnp.concatenate([jnp.concatenate(row, axis=1) for row in w], axis=0)
        w = pltpu.roll(w, base, 1)
        inside = (lane >= base) & (lane < base + width)
        eye = jnp.where(lane - base == sub, 1.0, 0.0).astype(jnp.float32)
        a_ref[...] = a_ref[...] - tn_narrow(panel, jnp.where(inside, eye + w, w))
        a_ref[pl.ds(base, width), :] = w
        return 0

    lax.fori_loop(0, n // width, step, 0)
    a_ref[...] = -a_ref[...]


def chain_kernel(local, scale, core_ref, here_ref, there_ref, dev_ref, r_ref, e_ref, v_ref, inv0, inv1, inv2, k_ref, t_ref, g_ref):
    p = r_ref.shape[1]
    first = core_ref[0] == 0
    eye = lax.broadcasted_iota(jnp.int32, (p, p), 0) == lax.broadcasted_iota(jnp.int32, (p, p), 1)

    def block(i, j):
        half, n = (0, HALF_A.index((i, j))) if (i, j) in HALF_A else (1, HALF_B.index((i, j)))
        mine, other = here_ref[n * p : (n + 1) * p, :], there_ref[n * p : (n + 1) * p, :]
        total = jnp.where(first, mine, other) if half == 0 else jnp.where(first, other, mine)
        between = tn_narrow(dev_ref[:, i * p : (i + 1) * p], dev_ref[:, j * p : (j + 1) * p])
        return (total + local * between) * scale

    def add_diag(x, n):
        return x + jnp.where(eye, r_ref[n : n + 1, :], 0.0)

    inv0[...] = add_diag(block(0, 0), 0)
    invert_in_place(inv0)
    k_ref[0:p, :] = mm(block(1, 0), inv0[...])
    k_ref[p : 2 * p, :] = mm(block(2, 0), inv0[...])
    g_ref[0] = block(3, 3)
    g_ref[1] = block(1, 3)
    g_ref[2] = block(2, 3)
    g_ref[3] = block(3, 4)
    kh = mm(k_ref[...], 0.5 * g_ref[0])
    t_ref[0:p, :] = g_ref[1] + kh[:p]
    t_ref[p : 2 * p, :] = g_ref[2] + kh[p:]
    t_ref[2 * p :, :] = g_ref[3].T - kh[:p]
    z1 = mm_nt(k_ref[0:p, :], t_ref[...])
    z2 = mm_nt(k_ref[p : 2 * p, :], t_ref[...])
    inv1[...] = add_diag(block(1, 1) + z1[:, :p] + z1[:, :p].T, 1)
    c21 = block(2, 1) + z2[:, :p] + z1[:, p : 2 * p].T
    c22 = block(2, 2) + z2[:, p : 2 * p] + z2[:, p : 2 * p].T
    ce2 = block(2, 4).T - z1[:, p : 2 * p] + z2[:, 2 * p :].T
    cee = block(4, 4) - z1[:, 2 * p :] - z1[:, 2 * p :].T
    t_ref[0:p, :] = ce2
    t_ref[p : 2 * p, :] = cee
    invert_in_place(inv1)
    k21 = mm(c21, inv1[...])
    kh = mm(k21, t_ref[p : 2 * p, :])
    z = mm_nt(k21, t_ref[0:p, :].T + 0.5 * kh)
    inv2[...] = add_diag(c22 + z + z.T, 2)
    invert_in_place(inv2)
    e0 = e_ref[0:p, :]
    ke = mm(k_ref[...], e0)
    e1 = e_ref[p : 2 * p, :] - ke[:p]
    e2 = e_ref[2 * p :, :] - ke[p:] - mm(k21, e1)
    w2 = mm(inv2[...], e2)
    v_ref[2 * p : 3 * p, :] = w2 * scale
    w1 = mm(inv1[...], e1 + mm(t_ref[0:p, :] + kh.T, w2))
    v_ref[p : 2 * p, :] = w1 * scale
    k21w2 = mm_tn(k21, w2)
    v_ref[4 * p :, :] = k21w2 * scale
    v3 = mm_tn(k_ref[0:p, :], w1 - k21w2) + mm_tn(k_ref[p : 2 * p, :], w2)
    v_ref[3 * p : 4 * p, :] = v3 * scale
    w0 = e0 + mm_tn(g_ref[1], w1) + mm_tn(g_ref[2], w2) + mm(g_ref[0], v3) + mm(g_ref[3], k21w2)
    v_ref[0:p, :] = mm(inv0[...], w0) * scale


def chain(core, here, there, dev, r, e, local, scale):
    p = r.shape[1]
    vm = pl.BlockSpec(memory_space=pltpu.VMEM)
    return pl.pallas_call(
        functools.partial(chain_kernel, local, scale),
        out_shape=jax.ShapeDtypeStruct((5 * p, e.shape[1]), jnp.float32),
        in_specs=[pl.BlockSpec(memory_space=pltpu.SMEM)] + [vm] * 5,
        out_specs=vm,
        scratch_shapes=[pltpu.VMEM((p, p), jnp.float32)] * 3
        + [pltpu.VMEM((2 * p, p), jnp.float32), pltpu.VMEM((3 * p, p), jnp.float32), pltpu.VMEM((4, p, p), jnp.float32)],
        name="chain",
    )(core, here, there, dev, r, e)


def prepare_kernel(core_ref, here_ref, there_ref, state_ref, pred_ref, inno_ref, cross_x_ref, cross_h_ref, pay_ref, y_ref):
    p, local = inno_ref.shape[0] // 3, inno_ref.shape[1]
    n_mem, part = pay_ref.shape[0], here_ref.shape[2] // 2
    first = core_ref[0] == 0
    for b in range(3):
        mine, other = here_ref[:, b], there_ref[:, b]
        even = jnp.where(first, mine, other)
        odd = jnp.where(first, other, mine)
        obs = jnp.concatenate([even[:, :part], odd[:, :part]], axis=1).reshape(p, local)
        pert = jnp.concatenate([even[:, part:], odd[:, part:]], axis=1).reshape(p, local)
        inno = pert - obs
        inno_ref[b * p : (b + 1) * p, :] = inno
        y_ref[b * p : (b + 1) * p, :] = obs
        if b < 2:
            y_ref[(3 + b) * p : (4 + b) * p, :] = inno
    ones = jnp.ones((TILE, local), jnp.float32)
    n_gram = 6 * p // n_mem
    row = n_gram

    def extra(values):
        nonlocal row
        for at in range(0, values.shape[1], p):
            piece = values[0:1, at : at + p]
            if piece.shape[1] < p:
                piece = jnp.concatenate([piece, jnp.zeros((1, p - piece.shape[1]), jnp.float32)], axis=1)
            pay_ref[:, row : row + 1, :] = jnp.broadcast_to(piece[None], (n_mem, 1, p))
            row += 1

    pay_ref[:, n_gram:, :] = jnp.zeros((n_mem, pay_ref.shape[1] - n_gram, p), jnp.float32)
    extra(mm_nt(ones, y_ref[...]) * (1.0 / local))
    extra(jnp.concatenate([mm_nt(ones, state_ref[...]), mm_nt(ones, pred_ref[...])], axis=1))
    for i in range(5):
        rows = y_ref[i * p : (i + 1) * p, :]
        y_ref[i * p : (i + 1) * p, :] = rows - jnp.sum(rows, axis=1, keepdims=True) * (1.0 / local)

    def products(pairs):
        for n, (i, j) in enumerate(pairs):
            block = mm_nt(y_ref[i * p : (i + 1) * p, :], y_ref[j * p : (j + 1) * p, :])
            at = 0
            while at < p:
                dest, off = divmod(n * p + at, n_gram)
                size = min(n_gram - off, p - at)
                pay_ref[dest, off : off + size, :] = block[at : at + size]
                at += size

    @pl.when(first)
    def _():
        products(HALF_A)

    @pl.when(jnp.logical_not(first))
    def _():
        products(HALF_B)

    for src_ref, out_ref in ((state_ref, cross_x_ref), (pred_ref, cross_h_ref)):
        chunk = 128

        def step(n, _, src_ref=src_ref, out_ref=out_ref):
            at = pl.ds(pl.multiple_of(n * chunk, chunk), chunk)
            out_ref[at, :] = mm_nt(src_ref[at, :], y_ref[...])
            return 0

        lax.fori_loop(0, src_ref.shape[0] // chunk, step, 0)


def prepare(core, here, there, state, predicted, n_mem):
    p, local = here.shape[0] * here.shape[2], state.shape[1]
    n_gram = 6 * p // n_mem
    n_extra = 5 + -(-(state.shape[0] + predicted.shape[0]) // p)
    vm = pl.BlockSpec(memory_space=pltpu.VMEM)
    return pl.pallas_call(
        prepare_kernel,
        out_shape=[
            jax.ShapeDtypeStruct((3 * p, local), jnp.float32),
            jax.ShapeDtypeStruct((state.shape[0], 5 * p), jnp.float32),
            jax.ShapeDtypeStruct((predicted.shape[0], 5 * p), jnp.float32),
            jax.ShapeDtypeStruct((n_mem, n_gram + -(-n_extra // TILE) * TILE, p), jnp.float32),
        ],
        in_specs=[pl.BlockSpec(memory_space=pltpu.SMEM)] + [vm] * 4,
        out_specs=[vm] * 4,
        scratch_shapes=[pltpu.VMEM((5 * p, local), jnp.float32)],
        name="prepare",
    )(core, here, there, state, predicted)


def make(n_rows, n_mem):
    cores = 2
    n_z = n_rows // cores
    same_core = [[z * cores + c for z in range(n_z)] for c in range(cores)]
    swap = [(i, i ^ 1) for i in range(n_rows)]

    def on_device(state, predicted, perturbed, obs_variance, owners, positions):
        p = positions.shape[1]
        local = state.shape[1]
        members = local * n_mem
        part = p // n_rows
        row = lax.axis_index("rows")
        core = row % cores

        mine = jnp.argmax(owners == row)
        picked = positions[mine]
        out = jnp.concatenate(
            [
                jnp.take(predicted, picked, axis=0).reshape(n_rows, part, local),
                jnp.take(perturbed, picked, axis=0).reshape(n_rows, part, local),
            ],
            axis=1,
        )
        got = lax.all_to_all(out, "rows", 0, 0, tiled=True)
        piece = jnp.take(got, owners, axis=0)
        here = lax.all_gather(piece, "rows", axis_index_groups=same_core)
        there = lax.ppermute(here, "rows", swap)
        which = core.reshape(1).astype(jnp.int32)
        inno, cross_x, cross_h, payload = prepare(which, here, there, state, predicted, n_mem)
        n_gram = 6 * p // n_mem
        n_state = state.shape[0] + predicted.shape[0]
        cross_x, cross_h = lax.psum((cross_x, cross_h), "mem")
        got = lax.all_to_all(payload, "mem", 0, 0, tiled=True)
        summed = jnp.sum(got[:, :n_gram], axis=0)
        extra = got[:, n_gram:].reshape(n_mem, -1)
        mu_all = extra[:, : 5 * p]
        sums_all = extra[:, 5 * p : 5 * p + n_state]
        here = lax.all_to_all(
            jnp.broadcast_to(summed[None], (n_mem, n_gram, p)), "mem", 0, 0, tiled=True
        ).reshape(6 * p, p)
        there = lax.ppermute(here, "rows", swap)
        dev = mu_all - jnp.sum(mu_all, axis=0, keepdims=True) / n_mem
        v = chain(
            which,
            here,
            there,
            dev,
            obs_variance,
            inno,
            float(local),
            1.0 / (members - 1),
        )
        between = mm(dev, v)
        n_x = state.shape[0]
        new_state = state + mm(cross_x, v) + mm_tn(sums_all[:, :n_x], between)
        new_obs = predicted + mm(cross_h, v) + mm_tn(sums_all[:, n_x:], between)
        return new_state, new_obs

    return on_device


def solution(mesh):
    in_specs = (P("rows", "mem"), P("rows", "mem"), P("rows", "mem"), P(), P(), P())
    out_specs = (P("rows", "mem"), P("rows", "mem"))
    inner = make(mesh.shape["rows"], mesh.shape["mem"])

    return jax.shard_map(
        inner,
        mesh=mesh,
        in_specs=in_specs,
        out_specs=out_specs,
        check_vma=False,
    )
```

```python
import functools

import jax
import jax.numpy as jnp
from jax import lax
from jax.experimental import pallas as pl
from jax.experimental.pallas import tpu as pltpu
from jax.sharding import PartitionSpec as P

exact = lax.Precision.HIGHEST
HALF_A = ((0, 0), (1, 0), (2, 0), (1, 1), (2, 1), (2, 2))
HALF_B = ((1, 3), (2, 3), (3, 3), (2, 4), (3, 4), (4, 4))


def mm(a, b):
    return lax.dot_general(a, b, (((1,), (0,)), ((), ())), precision=exact, preferred_element_type=jnp.float32)


def mm_nt(a, b):
    return lax.dot_general(a, b, (((1,), (1,)), ((), ())), precision=exact, preferred_element_type=jnp.float32)


def mm_tn(a, b):
    return lax.dot_general(a, b, (((0,), (0,)), ((), ())), precision=exact, preferred_element_type=jnp.float32)


TILE = 8
LANES = 128


def split3(x):
    hi = x.astype(jnp.bfloat16)
    rest = x - hi.astype(jnp.float32)
    mid = rest.astype(jnp.bfloat16)
    low = (rest - mid.astype(jnp.float32)).astype(jnp.bfloat16)
    return hi, mid, low


def tn_narrow(a, b):
    ah, am, al = split3(a)
    bh, bm, bl = split3(b)
    left = jnp.concatenate([ah, ah, am, ah, am, al], axis=0)
    right = jnp.concatenate([bh, bm, bh, bl, bm, bh], axis=0)
    return lax.dot_general(left, right, (((0,), (0,)), ((), ())), preferred_element_type=jnp.float32)


def sweep_tiles(w, width):
    lane = lax.broadcasted_iota(jnp.int32, (TILE, LANES), 1)
    sub = lax.broadcasted_iota(jnp.int32, (TILE, LANES), 0)
    full = (TILE, LANES)
    n = width // TILE
    for s in range(n):
        off = s * TILE
        own = (lane >= off) & (lane < off + TILE)
        eye = jnp.where(lane - off == sub, 1.0, 0.0).astype(jnp.float32)
        cols = [[jnp.broadcast_to(w[t][0][:, off + j : off + j + 1], full) for j in range(TILE)] for t in range(n)]
        c = {}
        for j in range(TILE):
            for i in range(j, TILE):
                c[i, j] = jnp.broadcast_to(cols[s][j][i : i + 1, :], full)
        get = lambda i, j: c[max(i, j), min(i, j)]
        for j in range(TILE):
            r = 1.0 / c[j, j]
            old = {i: get(i, j) for i in range(TILE) if i != j}
            scaled = {i: old[i] * r for i in old}
            for k in range(TILE):
                for i in range(k, TILE):
                    if i != j and k != j:
                        c[i, k] = c[i, k] - scaled[i] * old[k]
            for i in old:
                c[max(i, j), min(i, j)] = scaled[i]
            c[j, j] = -r
        tcol = []
        for j in range(TILE):
            col = get(0, j)
            for i in range(1, TILE):
                col = jnp.where(sub == i, get(i, j), col)
            tcol.append(-col)
        rows, alt = [], []
        for h in range(len(w[0])):
            bz = jnp.where(own, eye, w[s][h]) if h == 0 else w[s][h]
            acc = tcol[0] * jnp.broadcast_to(bz[0:1, :], full)
            for j in range(1, TILE):
                acc = acc + tcol[j] * jnp.broadcast_to(bz[j : j + 1, :], full)
            rows.append(jnp.where(own, -acc, acc) if h == 0 else acc)
            alt.append(jnp.where(own, eye - acc, acc) if h == 0 else acc)
        spread = [[jnp.broadcast_to(a[j : j + 1, :], full) for j in range(TILE)] for a in alt]
        for t in range(n):
            if t == s:
                w[t] = rows
                continue
            new = []
            for h in range(len(alt)):
                acc = cols[t][0] * spread[h][0]
                for j in range(1, TILE):
                    acc = acc + cols[t][j] * spread[h][j]
                new.append(w[t][h] - acc)
            w[t] = new
    return w


def invert_in_place(a_ref, width=32):
    n = a_ref.shape[0]
    lane = lax.broadcasted_iota(jnp.int32, (width, n), 1)
    sub = lax.broadcasted_iota(jnp.int32, (width, n), 0)

    def step(b, _):
        base = pl.multiple_of(b * width, width)
        panel = a_ref[pl.ds(base, width), :]
        rolled = pltpu.roll(panel, lax.rem(n - base, n), 1)
        w = [
            [rolled[t * TILE : (t + 1) * TILE, h * LANES : (h + 1) * LANES] for h in range(n // LANES)]
            for t in range(width // TILE)
        ]
        w = sweep_tiles(w, width)
        w = jnp.concatenate([jnp.concatenate(row, axis=1) for row in w], axis=0)
        w = pltpu.roll(w, base, 1)
        inside = (lane >= base) & (lane < base + width)
        eye = jnp.where(lane - base == sub, 1.0, 0.0).astype(jnp.float32)
        a_ref[...] = a_ref[...] - tn_narrow(panel, jnp.where(inside, eye + w, w))
        a_ref[pl.ds(base, width), :] = w
        return 0

    lax.fori_loop(0, n // width, step, 0)
    a_ref[...] = -a_ref[...]


def chain_kernel(local, scale, core_ref, here_ref, there_ref, dev_ref, r_ref, e_ref, v_ref, inv0, inv1, inv2, k_ref, t_ref, g_ref):
    p = r_ref.shape[1]
    first = core_ref[0] == 0
    eye = lax.broadcasted_iota(jnp.int32, (p, p), 0) == lax.broadcasted_iota(jnp.int32, (p, p), 1)

    def block(i, j):
        half, n = (0, HALF_A.index((i, j))) if (i, j) in HALF_A else (1, HALF_B.index((i, j)))
        mine, other = here_ref[n * p : (n + 1) * p, :], there_ref[n * p : (n + 1) * p, :]
        total = jnp.where(first, mine, other) if half == 0 else jnp.where(first, other, mine)
        between = tn_narrow(dev_ref[:, i * p : (i + 1) * p], dev_ref[:, j * p : (j + 1) * p])
        return (total + local * between) * scale

    def add_diag(x, n):
        return x + jnp.where(eye, r_ref[n : n + 1, :], 0.0)

    inv0[...] = add_diag(block(0, 0), 0)
    invert_in_place(inv0)
    k_ref[0:p, :] = mm(block(1, 0), inv0[...])
    k_ref[p : 2 * p, :] = mm(block(2, 0), inv0[...])
    g_ref[0] = block(3, 3)
    g_ref[1] = block(1, 3)
    g_ref[2] = block(2, 3)
    g_ref[3] = block(3, 4)
    kh = mm(k_ref[...], 0.5 * g_ref[0])
    t_ref[0:p, :] = g_ref[1] + kh[:p]
    t_ref[p : 2 * p, :] = g_ref[2] + kh[p:]
    t_ref[2 * p :, :] = g_ref[3].T - kh[:p]
    z1 = mm_nt(k_ref[0:p, :], t_ref[...])
    z2 = mm_nt(k_ref[p : 2 * p, :], t_ref[...])
    inv1[...] = add_diag(block(1, 1) + z1[:, :p] + z1[:, :p].T, 1)
    c21 = block(2, 1) + z2[:, :p] + z1[:, p : 2 * p].T
    c22 = block(2, 2) + z2[:, p : 2 * p] + z2[:, p : 2 * p].T
    ce2 = block(2, 4).T - z1[:, p : 2 * p] + z2[:, 2 * p :].T
    cee = block(4, 4) - z1[:, 2 * p :] - z1[:, 2 * p :].T
    t_ref[0:p, :] = ce2
    t_ref[p : 2 * p, :] = cee
    invert_in_place(inv1)
    k21 = mm(c21, inv1[...])
    kh = mm(k21, t_ref[p : 2 * p, :])
    z = mm_nt(k21, t_ref[0:p, :].T + 0.5 * kh)
    inv2[...] = add_diag(c22 + z + z.T, 2)
    invert_in_place(inv2)
    e0 = e_ref[0:p, :]
    ke = mm(k_ref[...], e0)
    e1 = e_ref[p : 2 * p, :] - ke[:p]
    e2 = e_ref[2 * p :, :] - ke[p:] - mm(k21, e1)
    w2 = mm(inv2[...], e2)
    v_ref[2 * p : 3 * p, :] = w2 * scale
    w1 = mm(inv1[...], e1 + mm(t_ref[0:p, :] + kh.T, w2))
    v_ref[p : 2 * p, :] = w1 * scale
    k21w2 = mm_tn(k21, w2)
    v_ref[4 * p :, :] = k21w2 * scale
    v3 = mm_tn(k_ref[0:p, :], w1 - k21w2) + mm_tn(k_ref[p : 2 * p, :], w2)
    v_ref[3 * p : 4 * p, :] = v3 * scale
    w0 = e0 + mm_tn(g_ref[1], w1) + mm_tn(g_ref[2], w2) + mm(g_ref[0], v3) + mm(g_ref[3], k21w2)
    v_ref[0:p, :] = mm(inv0[...], w0) * scale


def chain(core, here, there, dev, r, e, local, scale):
    p = r.shape[1]
    vm = pl.BlockSpec(memory_space=pltpu.VMEM)
    return pl.pallas_call(
        functools.partial(chain_kernel, local, scale),
        out_shape=jax.ShapeDtypeStruct((5 * p, e.shape[1]), jnp.float32),
        in_specs=[pl.BlockSpec(memory_space=pltpu.SMEM)] + [vm] * 5,
        out_specs=vm,
        scratch_shapes=[pltpu.VMEM((p, p), jnp.float32)] * 3
        + [pltpu.VMEM((2 * p, p), jnp.float32), pltpu.VMEM((3 * p, p), jnp.float32), pltpu.VMEM((4, p, p), jnp.float32)],
        name="chain",
    )(core, here, there, dev, r, e)


def pair(x, axis, order):
    hi = x.astype(jnp.bfloat16)
    low = (x - hi.astype(jnp.float32)).astype(jnp.bfloat16)
    return jnp.concatenate([(hi, low)[k] for k in order], axis=axis)


LEFT, RIGHT = (0, 0, 1), (0, 1, 0)


def dot3_nt(left, right):
    return lax.dot_general(left, right, (((1,), (1,)), ((), ())), preferred_element_type=jnp.float32)


def pick_kernel(row_ref, owners_ref, positions_ref, pred_ref, pert_ref, out_ref):
    part = out_ref.shape[1] // 2
    row = row_ref[0]
    mine = jnp.where(owners_ref[1] == row, 1, jnp.where(owners_ref[2] == row, 2, 0))

    def step(dest, _):
        for j in range(part):
            at = positions_ref[mine, dest * part + j]
            out_ref[dest, j : j + 1, :] = pred_ref[pl.ds(at, 1), :]
            out_ref[dest, part + j : part + j + 1, :] = pert_ref[pl.ds(at, 1), :]
        return 0

    lax.fori_loop(0, out_ref.shape[0], step, 0)


def pick(row, owners, positions, predicted, perturbed, n_rows):
    vm, sm = pl.BlockSpec(memory_space=pltpu.VMEM), pl.BlockSpec(memory_space=pltpu.SMEM)
    shape = (n_rows, 2 * positions.shape[1] // n_rows, predicted.shape[1])
    return pl.pallas_call(
        pick_kernel,
        out_shape=jax.ShapeDtypeStruct(shape, jnp.float32),
        in_specs=[sm, sm, sm, vm, vm],
        out_specs=vm,
        name="pick",
    )(row, owners, positions, predicted, perturbed)


def cross_kernel(core_ref, here_ref, there_ref, state_ref, pred_ref, inno_ref, y_ref, extra_ref, cross_x_ref, cross_h_ref, right_ref):
    p, local = inno_ref.shape[0] // 3, inno_ref.shape[1]
    part = here_ref.shape[2] // 2
    first = core_ref[0] == 0
    for b in range(3):
        mine, other = here_ref[:, b], there_ref[:, b]
        even = jnp.where(first, mine, other)
        odd = jnp.where(first, other, mine)
        obs = jnp.concatenate([even[:, :part], odd[:, :part]], axis=1).reshape(p, local)
        pert = jnp.concatenate([even[:, part:], odd[:, part:]], axis=1).reshape(p, local)
        inno = pert - obs
        inno_ref[b * p : (b + 1) * p, :] = inno
        y_ref[b * p : (b + 1) * p, :] = obs
        if b < 2:
            y_ref[(3 + b) * p : (4 + b) * p, :] = inno
    ones = jnp.ones((TILE, local), jnp.float32)
    row = 0
    extra_ref[...] = jnp.zeros(extra_ref.shape, jnp.float32)
    for source, factor in ((y_ref, 1.0 / local), (state_ref, 1.0), (pred_ref, 1.0)):
        values = mm_nt(ones, source[...]) * factor
        for at in range(0, values.shape[1], p):
            size = min(p, values.shape[1] - at)
            extra_ref[row : row + 1, 0:size] = values[0:1, at : at + size]
            row += 1
    for i in range(5):
        rows = y_ref[i * p : (i + 1) * p, :]
        rows = rows - jnp.sum(rows, axis=1, keepdims=True) * (1.0 / local)
        y_ref[i * p : (i + 1) * p, :] = rows
        right_ref[i * p : (i + 1) * p, :] = pair(rows, 1, RIGHT)
    chunk = 128
    for src_ref, out_ref in ((state_ref, cross_x_ref), (pred_ref, cross_h_ref)):

        def step(n, _, src_ref=src_ref, out_ref=out_ref):
            at = pl.ds(pl.multiple_of(n * chunk, chunk), chunk)
            out_ref[at, :] = dot3_nt(pair(src_ref[at, :], 1, LEFT), right_ref[...])
            return 0

        lax.fori_loop(0, src_ref.shape[0] // chunk, step, 0)


def extra_rows(p, *lengths):
    n = sum(-(-k // p) for k in lengths)
    return -(-n // TILE) * TILE


def cross_products(core, here, there, state, predicted):
    p, local = here.shape[0] * here.shape[2], state.shape[1]
    n_x, n_h = state.shape[0], predicted.shape[0]
    f32 = lambda *shape: jax.ShapeDtypeStruct(shape, jnp.float32)
    vm = pl.BlockSpec(memory_space=pltpu.VMEM)
    return pl.pallas_call(
        cross_kernel,
        out_shape=[
            f32(3 * p, local),
            f32(5 * p, local),
            f32(extra_rows(p, 5 * p, n_x, n_h), p),
            f32(n_x, 5 * p),
            f32(n_h, 5 * p),
        ],
        in_specs=[pl.BlockSpec(memory_space=pltpu.SMEM)] + [vm] * 4,
        out_specs=[vm] * 5,
        scratch_shapes=[pltpu.VMEM((5 * p, 3 * local), jnp.bfloat16)],
        name="cross",
    )(core, here, there, state, predicted)


def gram_kernel(core_ref, y_ref, extra_ref, pay_ref):
    n_mem, p = pay_ref.shape[0], pay_ref.shape[2]
    n_gram = 6 * p // n_mem
    pay_ref[:, n_gram:, :] = jnp.broadcast_to(extra_ref[...][None], (n_mem, *extra_ref.shape))

    def products(pairs):
        for n, (i, j) in enumerate(pairs):
            left = pair(y_ref[i * p : (i + 1) * p, :], 1, LEFT)
            block = dot3_nt(left, pair(y_ref[j * p : (j + 1) * p, :], 1, RIGHT))
            at = 0
            while at < p:
                dest, off = divmod(n * p + at, n_gram)
                size = min(n_gram - off, p - at)
                pay_ref[dest, off : off + size, :] = block[at : at + size]
                at += size

    @pl.when(core_ref[0] == 0)
    def _():
        products(HALF_A)

    @pl.when(core_ref[0] != 0)
    def _():
        products(HALF_B)


def gram_payload(core, y, extra, n_mem):
    p = extra.shape[1]
    vm = pl.BlockSpec(memory_space=pltpu.VMEM)
    return pl.pallas_call(
        gram_kernel,
        out_shape=jax.ShapeDtypeStruct((n_mem, 6 * p // n_mem + extra.shape[0], p), jnp.float32),
        in_specs=[pl.BlockSpec(memory_space=pltpu.SMEM), vm, vm],
        out_specs=vm,
        name="gram",
    )(core, y, extra)


def update_kernel(steps_x, state_ref, pred_ref, cross_x_ref, cross_h_ref, sums_ref, dev_ref, v_ref, new_x_ref, new_h_ref, right_ref, between_ref):
    n = pl.program_id(0)

    @pl.when(n == 0)
    def _():
        right_ref[...] = pair(v_ref[...], 0, RIGHT)
        between_ref[...] = mm(dev_ref[...], v_ref[...])

    def one(old_ref, cross_ref, new_ref):
        step = lax.dot_general(
            pair(cross_ref[...], 1, LEFT), right_ref[...], (((1,), (0,)), ((), ())), preferred_element_type=jnp.float32
        )
        new_ref[...] = old_ref[...] + (step + tn_narrow(sums_ref[...], between_ref[...]))

    @pl.when(n < steps_x)
    def _():
        one(state_ref, cross_x_ref, new_x_ref)

    @pl.when(n >= steps_x)
    def _():
        one(pred_ref, cross_h_ref, new_h_ref)


def update(state, predicted, cross_x, cross_h, sums, dev, v):
    chunk = 128
    local, wide = state.shape[1], cross_x.shape[1]
    steps_x, steps_h = state.shape[0] // chunk, predicted.shape[0] // chunk
    at_x = lambda n: (jnp.minimum(n, steps_x - 1), 0)
    at_h = lambda n: (jnp.maximum(n - steps_x, 0), 0)
    whole = lambda n: (0, 0)
    return pl.pallas_call(
        functools.partial(update_kernel, steps_x),
        grid=(steps_x + steps_h,),
        out_shape=[
            jax.ShapeDtypeStruct(state.shape, jnp.float32),
            jax.ShapeDtypeStruct(predicted.shape, jnp.float32),
        ],
        in_specs=[
            pl.BlockSpec((chunk, local), at_x),
            pl.BlockSpec((chunk, local), at_h),
            pl.BlockSpec((chunk, wide), at_x),
            pl.BlockSpec((chunk, wide), at_h),
            pl.BlockSpec((sums.shape[0], chunk), lambda n: (0, n)),
            pl.BlockSpec(dev.shape, whole),
            pl.BlockSpec(v.shape, whole),
        ],
        out_specs=[pl.BlockSpec((chunk, local), at_x), pl.BlockSpec((chunk, local), at_h)],
        scratch_shapes=[pltpu.VMEM((3 * wide, local), jnp.bfloat16), pltpu.VMEM((dev.shape[0], local), jnp.float32)],
        name="update",
    )(state, predicted, cross_x, cross_h, sums, dev, v)


def make(n_rows, n_mem):
    cores = 2
    n_z = n_rows // cores
    same_core = [[z * cores + c for z in range(n_z)] for c in range(cores)]
    swap = [(i, i ^ 1) for i in range(n_rows)]

    def on_device(state, predicted, perturbed, obs_variance, owners, positions):
        p = positions.shape[1]
        local = state.shape[1]
        members = local * n_mem
        row = lax.axis_index("rows")
        core = row % cores

        which = core.reshape(1).astype(jnp.int32)
        out = pick(row.reshape(1).astype(jnp.int32), owners, positions, predicted, perturbed, n_rows)
        got = lax.all_to_all(out, "rows", 0, 0, tiled=True)
        piece = jnp.take(got, owners, axis=0)
        here = lax.all_gather(piece, "rows", axis_index_groups=same_core)
        there = lax.ppermute(here, "rows", swap)
        inno, y, extra, cross_x, cross_h = cross_products(which, here, there, state, predicted)
        n_gram = 6 * p // n_mem
        cross_x, cross_h = lax.psum((cross_x, cross_h), "mem")
        payload = gram_payload(which, y, extra, n_mem)
        got = lax.all_to_all(payload, "mem", 0, 0, tiled=True)
        summed = jnp.sum(got[:, :n_gram], axis=0)
        extra = got[:, n_gram:].reshape(n_mem, -1)
        mu_all = extra[:, : 5 * p]
        n_x = -(-state.shape[0] // p) * p
        sums_all = jnp.concatenate(
            [extra[:, 5 * p : 5 * p + state.shape[0]], extra[:, 5 * p + n_x : 5 * p + n_x + predicted.shape[0]]], axis=1
        )
        here = lax.all_to_all(
            jnp.broadcast_to(summed[None], (n_mem, n_gram, p)), "mem", 0, 0, tiled=True
        ).reshape(6 * p, p)
        there = lax.ppermute(here, "rows", swap)
        dev = mu_all - jnp.sum(mu_all, axis=0, keepdims=True) / n_mem
        v = chain(
            which,
            here,
            there,
            dev,
            obs_variance,
            inno,
            float(local),
            1.0 / (members - 1),
        )
        return update(state, predicted, cross_x, cross_h, sums_all, dev, v)

    return on_device


def solution(mesh):
    in_specs = (P("rows", "mem"), P("rows", "mem"), P("rows", "mem"), P(), P(), P())
    out_specs = (P("rows", "mem"), P("rows", "mem"))
    inner = make(mesh.shape["rows"], mesh.shape["mem"])

    return jax.shard_map(
        inner,
        mesh=mesh,
        in_specs=in_specs,
        out_specs=out_specs,
        check_vma=False,
    )
```

```python
import functools

import jax
import jax.numpy as jnp
from jax import lax
from jax.experimental import pallas as pl
from jax.experimental.pallas import tpu as pltpu
from jax.sharding import PartitionSpec as P

exact = lax.Precision.HIGHEST
HALF_A = ((0, 0), (1, 0), (2, 0), (1, 1), (2, 1), (2, 2))
HALF_B = ((1, 3), (2, 3), (3, 3), (2, 4), (3, 4), (4, 4))


def mm(a, b):
    return lax.dot_general(a, b, (((1,), (0,)), ((), ())), precision=exact, preferred_element_type=jnp.float32)


def mm_nt(a, b):
    return lax.dot_general(a, b, (((1,), (1,)), ((), ())), precision=exact, preferred_element_type=jnp.float32)


def mm_tn(a, b):
    return lax.dot_general(a, b, (((0,), (0,)), ((), ())), precision=exact, preferred_element_type=jnp.float32)


TILE = 8
LANES = 128


def split3(x):
    hi = x.astype(jnp.bfloat16)
    rest = x - hi.astype(jnp.float32)
    mid = rest.astype(jnp.bfloat16)
    low = (rest - mid.astype(jnp.float32)).astype(jnp.bfloat16)
    return hi, mid, low


def tn_narrow(a, b):
    ah, am, al = split3(a)
    bh, bm, bl = split3(b)
    left = jnp.concatenate([ah, ah, am, ah, am, al], axis=0)
    right = jnp.concatenate([bh, bm, bh, bl, bm, bh], axis=0)
    return lax.dot_general(left, right, (((0,), (0,)), ((), ())), preferred_element_type=jnp.float32)


def sweep_tiles(w, width):
    lane = lax.broadcasted_iota(jnp.int32, (TILE, LANES), 1)
    sub = lax.broadcasted_iota(jnp.int32, (TILE, LANES), 0)
    full = (TILE, LANES)
    n = width // TILE
    for s in range(n):
        off = s * TILE
        own = (lane >= off) & (lane < off + TILE)
        eye = jnp.where(lane - off == sub, 1.0, 0.0).astype(jnp.float32)
        cols = [[jnp.broadcast_to(w[t][0][:, off + j : off + j + 1], full) for j in range(TILE)] for t in range(n)]
        c = {}
        for j in range(TILE):
            for i in range(j, TILE):
                c[i, j] = jnp.broadcast_to(cols[s][j][i : i + 1, :], full)
        get = lambda i, j: c[max(i, j), min(i, j)]
        for j in range(TILE):
            r = 1.0 / c[j, j]
            old = {i: get(i, j) for i in range(TILE) if i != j}
            scaled = {i: old[i] * r for i in old}
            for k in range(TILE):
                for i in range(k, TILE):
                    if i != j and k != j:
                        c[i, k] = c[i, k] - scaled[i] * old[k]
            for i in old:
                c[max(i, j), min(i, j)] = scaled[i]
            c[j, j] = -r
        tcol = []
        for j in range(TILE):
            col = get(0, j)
            for i in range(1, TILE):
                col = jnp.where(sub == i, get(i, j), col)
            tcol.append(-col)
        rows, alt = [], []
        for h in range(len(w[0])):
            bz = jnp.where(own, eye, w[s][h]) if h == 0 else w[s][h]
            acc = tcol[0] * jnp.broadcast_to(bz[0:1, :], full)
            for j in range(1, TILE):
                acc = acc + tcol[j] * jnp.broadcast_to(bz[j : j + 1, :], full)
            rows.append(jnp.where(own, -acc, acc) if h == 0 else acc)
            alt.append(jnp.where(own, eye - acc, acc) if h == 0 else acc)
        spread = [[jnp.broadcast_to(a[j : j + 1, :], full) for j in range(TILE)] for a in alt]
        for t in range(n):
            if t == s:
                w[t] = rows
                continue
            new = []
            for h in range(len(alt)):
                acc = cols[t][0] * spread[h][0]
                for j in range(1, TILE):
                    acc = acc + cols[t][j] * spread[h][j]
                new.append(w[t][h] - acc)
            w[t] = new
    return w


def invert_in_place(a_ref, width=32):
    n = a_ref.shape[0]
    lane = lax.broadcasted_iota(jnp.int32, (width, n), 1)
    sub = lax.broadcasted_iota(jnp.int32, (width, n), 0)

    def step(b, _):
        base = pl.multiple_of(b * width, width)
        panel = a_ref[pl.ds(base, width), :]
        rolled = pltpu.roll(panel, lax.rem(n - base, n), 1)
        w = [
            [rolled[t * TILE : (t + 1) * TILE, h * LANES : (h + 1) * LANES] for h in range(n // LANES)]
            for t in range(width // TILE)
        ]
        w = sweep_tiles(w, width)
        w = jnp.concatenate([jnp.concatenate(row, axis=1) for row in w], axis=0)
        w = pltpu.roll(w, base, 1)
        inside = (lane >= base) & (lane < base + width)
        eye = jnp.where(lane - base == sub, 1.0, 0.0).astype(jnp.float32)
        a_ref[...] = a_ref[...] - tn_narrow(panel, jnp.where(inside, eye + w, w))
        a_ref[pl.ds(base, width), :] = w
        return 0

    lax.fori_loop(0, n // width, step, 0)
    a_ref[...] = -a_ref[...]


def chain_kernel(local, scale, core_ref, here_ref, there_ref, dev_ref, r_ref, e_ref, v_ref, inv0, inv1, inv2, k_ref, t_ref, g_ref):
    p = r_ref.shape[1]
    first = core_ref[0] == 0
    eye = lax.broadcasted_iota(jnp.int32, (p, p), 0) == lax.broadcasted_iota(jnp.int32, (p, p), 1)

    def block(i, j):
        half, n = (0, HALF_A.index((i, j))) if (i, j) in HALF_A else (1, HALF_B.index((i, j)))
        mine, other = here_ref[n * p : (n + 1) * p, :], there_ref[n * p : (n + 1) * p, :]
        total = jnp.where(first, mine, other) if half == 0 else jnp.where(first, other, mine)
        between = tn_narrow(dev_ref[:, i * p : (i + 1) * p], dev_ref[:, j * p : (j + 1) * p])
        return (total + local * between) * scale

    def add_diag(x, n):
        return x + jnp.where(eye, r_ref[n : n + 1, :], 0.0)

    inv0[...] = add_diag(block(0, 0), 0)
    invert_in_place(inv0)
    k_ref[0:p, :] = mm(block(1, 0), inv0[...])
    k_ref[p : 2 * p, :] = mm(block(2, 0), inv0[...])
    g_ref[0] = block(3, 3)
    g_ref[1] = block(1, 3)
    g_ref[2] = block(2, 3)
    g_ref[3] = block(3, 4)
    kh = mm(k_ref[...], 0.5 * g_ref[0])
    t_ref[0:p, :] = g_ref[1] + kh[:p]
    t_ref[p : 2 * p, :] = g_ref[2] + kh[p:]
    t_ref[2 * p :, :] = g_ref[3].T - kh[:p]
    z1 = mm_nt(k_ref[0:p, :], t_ref[...])
    z2 = mm_nt(k_ref[p : 2 * p, :], t_ref[...])
    inv1[...] = add_diag(block(1, 1) + z1[:, :p] + z1[:, :p].T, 1)
    c21 = block(2, 1) + z2[:, :p] + z1[:, p : 2 * p].T
    c22 = block(2, 2) + z2[:, p : 2 * p] + z2[:, p : 2 * p].T
    ce2 = block(2, 4).T - z1[:, p : 2 * p] + z2[:, 2 * p :].T
    cee = block(4, 4) - z1[:, 2 * p :] - z1[:, 2 * p :].T
    t_ref[0:p, :] = ce2
    t_ref[p : 2 * p, :] = cee
    invert_in_place(inv1)
    k21 = mm(c21, inv1[...])
    kh = mm(k21, t_ref[p : 2 * p, :])
    z = mm_nt(k21, t_ref[0:p, :].T + 0.5 * kh)
    inv2[...] = add_diag(c22 + z + z.T, 2)
    invert_in_place(inv2)
    e0 = e_ref[0:p, :]
    ke = mm(k_ref[...], e0)
    e1 = e_ref[p : 2 * p, :] - ke[:p]
    e2 = e_ref[2 * p :, :] - ke[p:] - mm(k21, e1)
    w2 = mm(inv2[...], e2)
    v_ref[2 * p : 3 * p, :] = w2 * scale
    w1 = mm(inv1[...], e1 + mm(t_ref[0:p, :] + kh.T, w2))
    v_ref[p : 2 * p, :] = w1 * scale
    k21w2 = mm_tn(k21, w2)
    v_ref[4 * p :, :] = k21w2 * scale
    v3 = mm_tn(k_ref[0:p, :], w1 - k21w2) + mm_tn(k_ref[p : 2 * p, :], w2)
    v_ref[3 * p : 4 * p, :] = v3 * scale
    w0 = e0 + mm_tn(g_ref[1], w1) + mm_tn(g_ref[2], w2) + mm(g_ref[0], v3) + mm(g_ref[3], k21w2)
    v_ref[0:p, :] = mm(inv0[...], w0) * scale


def chain(core, here, there, dev, r, e, local, scale):
    p = r.shape[1]
    vm = pl.BlockSpec(memory_space=pltpu.VMEM)
    return pl.pallas_call(
        functools.partial(chain_kernel, local, scale),
        out_shape=jax.ShapeDtypeStruct((5 * p, e.shape[1]), jnp.float32),
        in_specs=[pl.BlockSpec(memory_space=pltpu.SMEM)] + [vm] * 5,
        out_specs=vm,
        scratch_shapes=[pltpu.VMEM((p, p), jnp.float32)] * 3
        + [pltpu.VMEM((2 * p, p), jnp.float32), pltpu.VMEM((3 * p, p), jnp.float32), pltpu.VMEM((4, p, p), jnp.float32)],
        name="chain",
    )(core, here, there, dev, r, e)


def pair(x, axis, order):
    hi = x.astype(jnp.bfloat16)
    low = (x - hi.astype(jnp.float32)).astype(jnp.bfloat16)
    return jnp.concatenate([(hi, low)[k] for k in order], axis=axis)


LEFT, RIGHT = (0, 0, 1), (0, 1, 0)
STEPS = 2


def dot3_nt(left, right):
    return lax.dot_general(left, right, (((1,), (1,)), ((), ())), preferred_element_type=jnp.float32)


def pick_kernel(row_ref, owners_ref, positions_ref, pred_ref, pert_ref, out_ref):
    part = out_ref.shape[1] // 2
    row = row_ref[0]
    mine = jnp.where(owners_ref[1] == row, 1, jnp.where(owners_ref[2] == row, 2, 0))

    def step(dest, _):
        for j in range(part):
            at = positions_ref[mine, dest * part + j]
            out_ref[dest, j : j + 1, :] = pred_ref[pl.ds(at, 1), :]
            out_ref[dest, part + j : part + j + 1, :] = pert_ref[pl.ds(at, 1), :]
        return 0

    lax.fori_loop(0, out_ref.shape[0], step, 0)


def pick(row, owners, positions, predicted, perturbed, n_rows):
    vm, sm = pl.BlockSpec(memory_space=pltpu.VMEM), pl.BlockSpec(memory_space=pltpu.SMEM)
    shape = (n_rows, 2 * positions.shape[1] // n_rows, predicted.shape[1])
    return pl.pallas_call(
        pick_kernel,
        out_shape=jax.ShapeDtypeStruct(shape, jnp.float32),
        in_specs=[sm, sm, sm, vm, vm],
        out_specs=vm,
        name="pick",
    )(row, owners, positions, predicted, perturbed)


def cross_kernel(core_ref, here_ref, there_ref, state_ref, pred_ref, inno_ref, y_ref, cross_x_ref, cross_h_ref, left_ref, right_ref):
    p, local = inno_ref.shape[0] // 3, inno_ref.shape[1]
    part = here_ref.shape[2] // 2
    n_x = state_ref.shape[0]
    first = core_ref[0] == 0
    for b in range(3):
        mine, other = here_ref[:, b], there_ref[:, b]
        even = jnp.where(first, mine, other)
        odd = jnp.where(first, other, mine)
        obs = jnp.concatenate([even[:, :part], odd[:, :part]], axis=1).reshape(p, local)
        pert = jnp.concatenate([even[:, part:], odd[:, part:]], axis=1).reshape(p, local)
        inno = pert - obs
        inno_ref[b * p : (b + 1) * p, :] = inno
        y_ref[b * p : (b + 1) * p, :] = obs
        right_ref[b * p : (b + 1) * p, :] = pair(centred(obs), 1, RIGHT)
        if b < 2:
            y_ref[(3 + b) * p : (4 + b) * p, :] = inno
            right_ref[(3 + b) * p : (4 + b) * p, :] = pair(centred(inno), 1, RIGHT)
    left_ref[:n_x, :] = pair(state_ref[...], 1, LEFT)
    left_ref[n_x:, :] = pair(pred_ref[...], 1, LEFT)

    def step(n, _):
        at = pl.ds(pl.multiple_of(n * p, p), p)
        block = dot3_nt(left_ref[...], right_ref[at, :])
        cross_x_ref[:, at] = block[:n_x]
        cross_h_ref[:, at] = block[n_x:]
        return 0

    lax.fori_loop(0, 5, step, 0)


def centred(rows):
    return rows - jnp.sum(rows, axis=1, keepdims=True) * (1.0 / rows.shape[1])


def extra_rows(p, *lengths):
    n = sum(-(-k // p) for k in lengths)
    return -(-n // TILE) * TILE


def cross_products(core, here, there, state, predicted):
    p, local = here.shape[0] * here.shape[2], state.shape[1]
    n_x, n_h = state.shape[0], predicted.shape[0]
    f32 = lambda *shape: jax.ShapeDtypeStruct(shape, jnp.float32)
    vm = pl.BlockSpec(memory_space=pltpu.VMEM)
    return pl.pallas_call(
        cross_kernel,
        out_shape=[f32(3 * p, local), f32(5 * p, local), f32(n_x, 5 * p), f32(n_h, 5 * p)],
        in_specs=[pl.BlockSpec(memory_space=pltpu.SMEM)] + [vm] * 4,
        out_specs=[vm] * 4,
        scratch_shapes=[pltpu.VMEM((n_x + n_h, 3 * local), jnp.bfloat16), pltpu.VMEM((5 * p, 3 * local), jnp.bfloat16)],
        name="cross",
    )(core, here, there, state, predicted)


def gram_kernel(core_ref, raw_ref, state_ref, pred_ref, pay_ref, y_ref, extra_ref):
    n_mem, p, local = pay_ref.shape[0], pay_ref.shape[2], raw_ref.shape[1]
    n_gram = 6 * p // n_mem
    ones = jnp.ones((TILE, local), jnp.float32)
    row = 0
    extra_ref[...] = jnp.zeros(extra_ref.shape, jnp.float32)
    for source, factor in ((raw_ref, 1.0 / local), (state_ref, 1.0), (pred_ref, 1.0)):
        values = mm_nt(ones, source[...]) * factor
        for at in range(0, values.shape[1], p):
            size = min(p, values.shape[1] - at)
            extra_ref[row : row + 1, 0:size] = values[0:1, at : at + size]
            row += 1
    for i in range(5):
        y_ref[i * p : (i + 1) * p, :] = centred(raw_ref[i * p : (i + 1) * p, :])
    pay_ref[:, n_gram:, :] = jnp.broadcast_to(extra_ref[...][None], (n_mem, *extra_ref.shape))

    def products(pairs):
        for n, (i, j) in enumerate(pairs):
            left = pair(y_ref[i * p : (i + 1) * p, :], 1, LEFT)
            block = dot3_nt(left, pair(y_ref[j * p : (j + 1) * p, :], 1, RIGHT))
            at = 0
            while at < p:
                dest, off = divmod(n * p + at, n_gram)
                size = min(n_gram - off, p - at)
                pay_ref[dest, off : off + size, :] = block[at : at + size]
                at += size

    @pl.when(core_ref[0] == 0)
    def _():
        products(HALF_A)

    @pl.when(core_ref[0] != 0)
    def _():
        products(HALF_B)


def gram_payload(core, y, state, predicted, p, n_mem):
    n_extra = extra_rows(p, y.shape[0], state.shape[0], predicted.shape[0])
    vm = pl.BlockSpec(memory_space=pltpu.VMEM)
    return pl.pallas_call(
        gram_kernel,
        out_shape=jax.ShapeDtypeStruct((n_mem, 6 * p // n_mem + n_extra, p), jnp.float32),
        in_specs=[pl.BlockSpec(memory_space=pltpu.SMEM), vm, vm, vm],
        out_specs=vm,
        scratch_shapes=[pltpu.VMEM(y.shape, jnp.float32), pltpu.VMEM((n_extra, p), jnp.float32)],
        name="gram",
    )(core, y, state, predicted)


def base_kernel(state_ref, pred_ref, sums_ref, dev_ref, v_ref, base_x_ref, base_h_ref, right_ref):
    n_x = state_ref.shape[0]
    wide = v_ref.shape[0] // STEPS
    dev = pair(dev_ref[...], 1, LEFT)
    right = pair(v_ref[...], 0, RIGHT)
    between = lax.dot_general(dev, right, (((1,), (0,)), ((), ())), preferred_element_type=jnp.float32)
    between = tn_narrow(sums_ref[...], between)
    base_x_ref[...] = state_ref[...] + between[:n_x]
    base_h_ref[...] = pred_ref[...] + between[n_x:]
    for n in range(STEPS):
        right_ref[3 * n * wide : 3 * (n + 1) * wide, :] = pair(v_ref[n * wide : (n + 1) * wide, :], 0, RIGHT)


def update_kernel(base_x_ref, base_h_ref, cross_x_ref, cross_h_ref, right_ref, new_x_ref, new_h_ref):
    n_x = base_x_ref.shape[0]

    @pl.when(pl.program_id(0) == 0)
    def _():
        new_x_ref[...] = base_x_ref[...]
        new_h_ref[...] = base_h_ref[...]

    left = jnp.concatenate([pair(cross_x_ref[...], 1, LEFT), pair(cross_h_ref[...], 1, LEFT)], axis=0)
    step = lax.dot_general(left, right_ref[...], (((1,), (0,)), ((), ())), preferred_element_type=jnp.float32)
    new_x_ref[...] = new_x_ref[...] + step[:n_x]
    new_h_ref[...] = new_h_ref[...] + step[n_x:]


def base_of(state, predicted, sums, dev, v):
    vm = pl.BlockSpec(memory_space=pltpu.VMEM)
    return pl.pallas_call(
        base_kernel,
        out_shape=[
            jax.ShapeDtypeStruct(state.shape, jnp.float32),
            jax.ShapeDtypeStruct(predicted.shape, jnp.float32),
            jax.ShapeDtypeStruct((3 * v.shape[0], v.shape[1]), jnp.bfloat16),
        ],
        in_specs=[vm] * 5,
        out_specs=[vm] * 3,
        name="base",
    )(state, predicted, sums, dev, v)


def update(base_x, base_h, cross_x, cross_h, right):
    local = base_x.shape[1]
    n_x, n_h = base_x.shape[0], base_h.shape[0]
    wide = cross_x.shape[1] // STEPS
    whole = lambda n: (0, 0)
    return pl.pallas_call(
        update_kernel,
        grid=(STEPS,),
        out_shape=[
            jax.ShapeDtypeStruct(base_x.shape, jnp.float32),
            jax.ShapeDtypeStruct(base_h.shape, jnp.float32),
        ],
        in_specs=[
            pl.BlockSpec(base_x.shape, whole),
            pl.BlockSpec(base_h.shape, whole),
            pl.BlockSpec((n_x, wide), lambda n: (0, n)),
            pl.BlockSpec((n_h, wide), lambda n: (0, n)),
            pl.BlockSpec((3 * wide, local), lambda n: (n, 0)),
        ],
        out_specs=[pl.BlockSpec(base_x.shape, whole), pl.BlockSpec(base_h.shape, whole)],
        name="update",
    )(base_x, base_h, cross_x, cross_h, right)


def make(n_rows, n_mem):
    cores = 2
    n_z = n_rows // cores
    same_core = [[z * cores + c for z in range(n_z)] for c in range(cores)]
    swap = [(i, i ^ 1) for i in range(n_rows)]

    def on_device(state, predicted, perturbed, obs_variance, owners, positions):
        p = positions.shape[1]
        local = state.shape[1]
        members = local * n_mem
        row = lax.axis_index("rows")
        core = row % cores

        which = core.reshape(1).astype(jnp.int32)
        out = pick(row.reshape(1).astype(jnp.int32), owners, positions, predicted, perturbed, n_rows)
        got = lax.all_to_all(out, "rows", 0, 0, tiled=True)
        piece = jnp.take(got, owners, axis=0)
        here = lax.all_gather(piece, "rows", axis_index_groups=same_core)
        there = lax.ppermute(here, "rows", swap)
        inno, y, cross_x, cross_h = cross_products(which, here, there, state, predicted)
        n_gram = 6 * p // n_mem
        cross_x, cross_h = lax.psum((cross_x, cross_h), "mem")
        payload = gram_payload(which, y, state, predicted, p, n_mem)
        got = lax.all_to_all(payload, "mem", 0, 0, tiled=True)
        summed = jnp.sum(got[:, :n_gram], axis=0)
        extra = got[:, n_gram:].reshape(n_mem, -1)
        mu_all = extra[:, : 5 * p]
        n_x = -(-state.shape[0] // p) * p
        sums_all = jnp.concatenate(
            [extra[:, 5 * p : 5 * p + state.shape[0]], extra[:, 5 * p + n_x : 5 * p + n_x + predicted.shape[0]]], axis=1
        )
        here = lax.all_to_all(
            jnp.broadcast_to(summed[None], (n_mem, n_gram, p)), "mem", 0, 0, tiled=True
        ).reshape(6 * p, p)
        there = lax.ppermute(here, "rows", swap)
        dev = mu_all - jnp.sum(mu_all, axis=0, keepdims=True) / n_mem
        v = chain(
            which,
            here,
            there,
            dev,
            obs_variance,
            inno,
            float(local),
            1.0 / (members - 1),
        )
        base_x, base_h, right = base_of(state, predicted, sums_all, dev, v)
        return update(base_x, base_h, cross_x, cross_h, right)

    return on_device


def solution(mesh):
    in_specs = (P("rows", "mem"), P("rows", "mem"), P("rows", "mem"), P(), P(), P())
    out_specs = (P("rows", "mem"), P("rows", "mem"))
    inner = make(mesh.shape["rows"], mesh.shape["mem"])

    return jax.shard_map(
        inner,
        mesh=mesh,
        in_specs=in_specs,
        out_specs=out_specs,
        check_vma=False,
    )
```

```python
import functools

import jax
import jax.numpy as jnp
from jax import lax
from jax.experimental import pallas as pl
from jax.experimental.pallas import tpu as pltpu
from jax.sharding import PartitionSpec as P

exact = lax.Precision.HIGHEST
HALF_A = ((0, 0), (1, 0), (2, 0), (1, 1), (2, 1), (2, 2))
HALF_B = ((1, 3), (2, 3), (3, 3), (2, 4), (3, 4), (4, 4))


def mm(a, b):
    return lax.dot_general(a, b, (((1,), (0,)), ((), ())), precision=exact, preferred_element_type=jnp.float32)


def mm_nt(a, b):
    return lax.dot_general(a, b, (((1,), (1,)), ((), ())), precision=exact, preferred_element_type=jnp.float32)


def mm_tn(a, b):
    return lax.dot_general(a, b, (((0,), (0,)), ((), ())), precision=exact, preferred_element_type=jnp.float32)


TILE = 8
LANES = 128


def split3(x):
    hi = x.astype(jnp.bfloat16)
    rest = x - hi.astype(jnp.float32)
    mid = rest.astype(jnp.bfloat16)
    low = (rest - mid.astype(jnp.float32)).astype(jnp.bfloat16)
    return hi, mid, low


def tn_narrow(a, b):
    ah, am, al = split3(a)
    bh, bm, bl = split3(b)
    left = jnp.concatenate([ah, ah, am, ah, am, al], axis=0)
    right = jnp.concatenate([bh, bm, bh, bl, bm, bh], axis=0)
    return lax.dot_general(left, right, (((0,), (0,)), ((), ())), preferred_element_type=jnp.float32)


def sweep_tiles(w, width):
    lane = lax.broadcasted_iota(jnp.int32, (TILE, LANES), 1)
    sub = lax.broadcasted_iota(jnp.int32, (TILE, LANES), 0)
    full = (TILE, LANES)
    n = width // TILE
    for s in range(n):
        off = s * TILE
        own = (lane >= off) & (lane < off + TILE)
        eye = jnp.where(lane - off == sub, 1.0, 0.0).astype(jnp.float32)
        cols = [[jnp.broadcast_to(w[t][0][:, off + j : off + j + 1], full) for j in range(TILE)] for t in range(n)]
        c = {}
        for j in range(TILE):
            for i in range(j, TILE):
                c[i, j] = jnp.broadcast_to(cols[s][j][i : i + 1, :], full)
        get = lambda i, j: c[max(i, j), min(i, j)]
        for j in range(TILE):
            r = 1.0 / c[j, j]
            old = {i: get(i, j) for i in range(TILE) if i != j}
            scaled = {i: old[i] * r for i in old}
            for k in range(TILE):
                for i in range(k, TILE):
                    if i != j and k != j:
                        c[i, k] = c[i, k] - scaled[i] * old[k]
            for i in old:
                c[max(i, j), min(i, j)] = scaled[i]
            c[j, j] = -r
        tcol = []
        for j in range(TILE):
            col = get(0, j)
            for i in range(1, TILE):
                col = jnp.where(sub == i, get(i, j), col)
            tcol.append(-col)
        rows, alt = [], []
        for h in range(len(w[0])):
            bz = jnp.where(own, eye, w[s][h]) if h == 0 else w[s][h]
            acc = tcol[0] * jnp.broadcast_to(bz[0:1, :], full)
            for j in range(1, TILE):
                acc = acc + tcol[j] * jnp.broadcast_to(bz[j : j + 1, :], full)
            rows.append(jnp.where(own, -acc, acc) if h == 0 else acc)
            alt.append(jnp.where(own, eye - acc, acc) if h == 0 else acc)
        spread = [[jnp.broadcast_to(a[j : j + 1, :], full) for j in range(TILE)] for a in alt]
        for t in range(n):
            if t == s:
                w[t] = rows
                continue
            new = []
            for h in range(len(alt)):
                acc = cols[t][0] * spread[h][0]
                for j in range(1, TILE):
                    acc = acc + cols[t][j] * spread[h][j]
                new.append(w[t][h] - acc)
            w[t] = new
    return w


def invert_in_place(a_ref, width=32):
    n = a_ref.shape[0]
    lane = lax.broadcasted_iota(jnp.int32, (width, n), 1)
    sub = lax.broadcasted_iota(jnp.int32, (width, n), 0)

    def step(b, _):
        base = pl.multiple_of(b * width, width)
        panel = a_ref[pl.ds(base, width), :]
        rolled = pltpu.roll(panel, lax.rem(n - base, n), 1)
        w = [
            [rolled[t * TILE : (t + 1) * TILE, h * LANES : (h + 1) * LANES] for h in range(n // LANES)]
            for t in range(width // TILE)
        ]
        w = sweep_tiles(w, width)
        w = jnp.concatenate([jnp.concatenate(row, axis=1) for row in w], axis=0)
        w = pltpu.roll(w, base, 1)
        inside = (lane >= base) & (lane < base + width)
        eye = jnp.where(lane - base == sub, 1.0, 0.0).astype(jnp.float32)
        a_ref[...] = a_ref[...] - tn_narrow(panel, jnp.where(inside, eye + w, w))
        a_ref[pl.ds(base, width), :] = w
        return 0

    lax.fori_loop(0, n // width, step, 0)
    a_ref[...] = -a_ref[...]


def chain_kernel(local, scale, core_ref, here_ref, there_ref, dev_ref, r_ref, e_ref, v_ref, inv0, inv1, inv2, k_ref, t_ref, g_ref):
    p = r_ref.shape[1]
    first = core_ref[0] == 0
    eye = lax.broadcasted_iota(jnp.int32, (p, p), 0) == lax.broadcasted_iota(jnp.int32, (p, p), 1)

    def block(i, j):
        half, n = (0, HALF_A.index((i, j))) if (i, j) in HALF_A else (1, HALF_B.index((i, j)))
        mine, other = here_ref[n * p : (n + 1) * p, :], there_ref[n * p : (n + 1) * p, :]
        total = jnp.where(first, mine, other) if half == 0 else jnp.where(first, other, mine)
        between = tn_narrow(dev_ref[:, i * p : (i + 1) * p], dev_ref[:, j * p : (j + 1) * p])
        return (total + local * between) * scale

    def add_diag(x, n):
        return x + jnp.where(eye, r_ref[n : n + 1, :], 0.0)

    inv0[...] = add_diag(block(0, 0), 0)
    invert_in_place(inv0)
    k_ref[0:p, :] = mm(block(1, 0), inv0[...])
    k_ref[p : 2 * p, :] = mm(block(2, 0), inv0[...])
    g_ref[0] = block(3, 3)
    g_ref[1] = block(1, 3)
    g_ref[2] = block(2, 3)
    g_ref[3] = block(3, 4)
    kh = mm(k_ref[...], 0.5 * g_ref[0])
    t_ref[0:p, :] = g_ref[1] + kh[:p]
    t_ref[p : 2 * p, :] = g_ref[2] + kh[p:]
    t_ref[2 * p :, :] = g_ref[3].T - kh[:p]
    z1 = mm_nt(k_ref[0:p, :], t_ref[...])
    z2 = mm_nt(k_ref[p : 2 * p, :], t_ref[...])
    inv1[...] = add_diag(block(1, 1) + z1[:, :p] + z1[:, :p].T, 1)
    c21 = block(2, 1) + z2[:, :p] + z1[:, p : 2 * p].T
    c22 = block(2, 2) + z2[:, p : 2 * p] + z2[:, p : 2 * p].T
    ce2 = block(2, 4).T - z1[:, p : 2 * p] + z2[:, 2 * p :].T
    cee = block(4, 4) - z1[:, 2 * p :] - z1[:, 2 * p :].T
    t_ref[0:p, :] = ce2
    t_ref[p : 2 * p, :] = cee
    invert_in_place(inv1)
    k21 = mm(c21, inv1[...])
    kh = mm(k21, t_ref[p : 2 * p, :])
    z = mm_nt(k21, t_ref[0:p, :].T + 0.5 * kh)
    inv2[...] = add_diag(c22 + z + z.T, 2)
    invert_in_place(inv2)
    e0 = e_ref[0:p, :]
    ke = mm(k_ref[...], e0)
    e1 = e_ref[p : 2 * p, :] - ke[:p]
    e2 = e_ref[2 * p :, :] - ke[p:] - mm(k21, e1)
    w2 = mm(inv2[...], e2)
    v_ref[2 * p : 3 * p, :] = w2 * scale
    w1 = mm(inv1[...], e1 + mm(t_ref[0:p, :] + kh.T, w2))
    v_ref[p : 2 * p, :] = w1 * scale
    k21w2 = mm_tn(k21, w2)
    v_ref[4 * p :, :] = k21w2 * scale
    v3 = mm_tn(k_ref[0:p, :], w1 - k21w2) + mm_tn(k_ref[p : 2 * p, :], w2)
    v_ref[3 * p : 4 * p, :] = v3 * scale
    w0 = e0 + mm_tn(g_ref[1], w1) + mm_tn(g_ref[2], w2) + mm(g_ref[0], v3) + mm(g_ref[3], k21w2)
    v_ref[0:p, :] = mm(inv0[...], w0) * scale


def chain(core, here, there, dev, r, e, local, scale):
    p = r.shape[1]
    vm = pl.BlockSpec(memory_space=pltpu.VMEM)
    return pl.pallas_call(
        functools.partial(chain_kernel, local, scale),
        out_shape=jax.ShapeDtypeStruct((5 * p, e.shape[1]), jnp.float32),
        in_specs=[pl.BlockSpec(memory_space=pltpu.SMEM)] + [vm] * 5,
        out_specs=vm,
        scratch_shapes=[pltpu.VMEM((p, p), jnp.float32)] * 3
        + [pltpu.VMEM((2 * p, p), jnp.float32), pltpu.VMEM((3 * p, p), jnp.float32), pltpu.VMEM((4, p, p), jnp.float32)],
        name="chain",
    )(core, here, there, dev, r, e)


def pair(x, axis, order):
    hi = x.astype(jnp.bfloat16)
    low = (x - hi.astype(jnp.float32)).astype(jnp.bfloat16)
    return jnp.concatenate([(hi, low)[k] for k in order], axis=axis)


LEFT, RIGHT = (0, 0, 1), (0, 1, 0)
STEPS = 2


def dot3_nt(left, right):
    return lax.dot_general(left, right, (((1,), (1,)), ((), ())), preferred_element_type=jnp.float32)


def pick_kernel(row_ref, owners_ref, positions_ref, pred_ref, pert_ref, out_ref):
    part = out_ref.shape[1] // 2
    row = row_ref[0]
    mine = jnp.where(owners_ref[1] == row, 1, jnp.where(owners_ref[2] == row, 2, 0))

    def step(dest, _):
        for j in range(part):
            at = positions_ref[mine, dest * part + j]
            out_ref[dest, j : j + 1, :] = pred_ref[pl.ds(at, 1), :]
            out_ref[dest, part + j : part + j + 1, :] = pert_ref[pl.ds(at, 1), :]
        return 0

    lax.fori_loop(0, out_ref.shape[0], step, 0)


def pick(row, owners, positions, predicted, perturbed, n_rows):
    vm, sm = pl.BlockSpec(memory_space=pltpu.VMEM), pl.BlockSpec(memory_space=pltpu.SMEM)
    shape = (n_rows, 2 * positions.shape[1] // n_rows, predicted.shape[1])
    return pl.pallas_call(
        pick_kernel,
        out_shape=jax.ShapeDtypeStruct(shape, jnp.float32),
        in_specs=[sm, sm, sm, vm, vm],
        out_specs=vm,
        name="pick",
    )(row, owners, positions, predicted, perturbed)


def cross_kernel(core_ref, here_ref, there_ref, state_ref, pred_ref, inno_ref, y_ref, cross_x_ref, cross_h_ref, left_ref, right_ref):
    p, local = inno_ref.shape[0] // 3, inno_ref.shape[1]
    part = here_ref.shape[2] // 2
    n_x = state_ref.shape[0]
    first = core_ref[0] == 0
    for b in range(3):
        mine, other = here_ref[:, b], there_ref[:, b]
        even = jnp.where(first, mine, other)
        odd = jnp.where(first, other, mine)
        obs = jnp.concatenate([even[:, :part], odd[:, :part]], axis=1).reshape(p, local)
        pert = jnp.concatenate([even[:, part:], odd[:, part:]], axis=1).reshape(p, local)
        inno = pert - obs
        inno_ref[b * p : (b + 1) * p, :] = inno
        y_ref[b * p : (b + 1) * p, :] = obs
        right_ref[b * p : (b + 1) * p, :] = pair(centred(obs), 1, RIGHT)
        if b < 2:
            y_ref[(3 + b) * p : (4 + b) * p, :] = inno
            right_ref[(3 + b) * p : (4 + b) * p, :] = pair(centred(inno), 1, RIGHT)
    left_ref[:n_x, :] = pair(state_ref[...], 1, LEFT)
    left_ref[n_x:, :] = pair(pred_ref[...], 1, LEFT)

    def step(n, _):
        at = pl.ds(pl.multiple_of(n * p, p), p)
        block = dot3_nt(left_ref[...], right_ref[at, :])
        cross_x_ref[:, at] = block[:n_x]
        cross_h_ref[:, at] = block[n_x:]
        return 0

    lax.fori_loop(0, 5, step, 0)


def centred(rows):
    return rows - jnp.sum(rows, axis=1, keepdims=True) * (1.0 / rows.shape[1])


def extra_rows(p, *lengths):
    n = sum(-(-k // p) for k in lengths)
    return -(-n // TILE) * TILE


def cross_products(core, here, there, state, predicted):
    p, local = here.shape[0] * here.shape[2], state.shape[1]
    n_x, n_h = state.shape[0], predicted.shape[0]
    f32 = lambda *shape: jax.ShapeDtypeStruct(shape, jnp.float32)
    vm = pl.BlockSpec(memory_space=pltpu.VMEM)
    return pl.pallas_call(
        cross_kernel,
        out_shape=[f32(3 * p, local), f32(5 * p, local), f32(n_x, 5 * p), f32(n_h, 5 * p)],
        in_specs=[pl.BlockSpec(memory_space=pltpu.SMEM)] + [vm] * 4,
        out_specs=[vm] * 4,
        scratch_shapes=[pltpu.VMEM((n_x + n_h, 3 * local), jnp.bfloat16), pltpu.VMEM((5 * p, 3 * local), jnp.bfloat16)],
        name="cross",
    )(core, here, there, state, predicted)


def gram_kernel(core_ref, raw_ref, state_ref, pred_ref, pay_ref, y_ref, extra_ref):
    n_mem, p, local = pay_ref.shape[0], pay_ref.shape[2], raw_ref.shape[1]
    n_gram = 6 * p // n_mem
    ones = jnp.ones((TILE, local), jnp.float32)
    row = 0
    extra_ref[...] = jnp.zeros(extra_ref.shape, jnp.float32)
    for source, factor in ((raw_ref, 1.0 / local), (state_ref, 1.0), (pred_ref, 1.0)):
        values = mm_nt(ones, source[...]) * factor
        for at in range(0, values.shape[1], p):
            size = min(p, values.shape[1] - at)
            extra_ref[row : row + 1, 0:size] = values[0:1, at : at + size]
            row += 1
    for i in range(5):
        y_ref[i * p : (i + 1) * p, :] = centred(raw_ref[i * p : (i + 1) * p, :])
    pay_ref[:, n_gram:, :] = jnp.broadcast_to(extra_ref[...][None], (n_mem, *extra_ref.shape))

    def products(pairs):
        for n, (i, j) in enumerate(pairs):
            left = pair(y_ref[i * p : (i + 1) * p, :], 1, LEFT)
            block = dot3_nt(left, pair(y_ref[j * p : (j + 1) * p, :], 1, RIGHT))
            at = 0
            while at < p:
                dest, off = divmod(n * p + at, n_gram)
                size = min(n_gram - off, p - at)
                pay_ref[dest, off : off + size, :] = block[at : at + size]
                at += size

    @pl.when(core_ref[0] == 0)
    def _():
        products(HALF_A)

    @pl.when(core_ref[0] != 0)
    def _():
        products(HALF_B)


def gram_payload(core, y, state, predicted, p, n_mem):
    n_extra = extra_rows(p, y.shape[0], state.shape[0], predicted.shape[0])
    vm = pl.BlockSpec(memory_space=pltpu.VMEM)
    return pl.pallas_call(
        gram_kernel,
        out_shape=jax.ShapeDtypeStruct((n_mem, 6 * p // n_mem + n_extra, p), jnp.float32),
        in_specs=[pl.BlockSpec(memory_space=pltpu.SMEM), vm, vm, vm],
        out_specs=vm,
        scratch_shapes=[pltpu.VMEM(y.shape, jnp.float32), pltpu.VMEM((n_extra, p), jnp.float32)],
        name="gram",
    )(core, y, state, predicted)


def base_kernel(state_ref, pred_ref, sums_ref, dev_ref, v_ref, base_x_ref, base_h_ref, right_ref):
    n_x = state_ref.shape[0]
    wide = v_ref.shape[0] // STEPS
    dev = pair(dev_ref[...], 1, LEFT)
    right = pair(v_ref[...], 0, RIGHT)
    between = lax.dot_general(dev, right, (((1,), (0,)), ((), ())), preferred_element_type=jnp.float32)
    between = tn_narrow(sums_ref[...], between)
    base_x_ref[...] = state_ref[...] + between[:n_x]
    base_h_ref[...] = pred_ref[...] + between[n_x:]
    for n in range(STEPS):
        right_ref[3 * n * wide : 3 * (n + 1) * wide, :] = pair(v_ref[n * wide : (n + 1) * wide, :], 0, RIGHT)


def update_kernel(base_x_ref, base_h_ref, cross_x_ref, cross_h_ref, right_ref, new_x_ref, new_h_ref):
    n_x = base_x_ref.shape[0]

    @pl.when(pl.program_id(0) == 0)
    def _():
        new_x_ref[...] = base_x_ref[...]
        new_h_ref[...] = base_h_ref[...]

    left = jnp.concatenate([pair(cross_x_ref[...], 1, LEFT), pair(cross_h_ref[...], 1, LEFT)], axis=0)
    step = lax.dot_general(left, right_ref[...], (((1,), (0,)), ((), ())), preferred_element_type=jnp.float32)
    new_x_ref[...] = new_x_ref[...] + step[:n_x]
    new_h_ref[...] = new_h_ref[...] + step[n_x:]


def base_of(state, predicted, sums, dev, v):
    vm = pl.BlockSpec(memory_space=pltpu.VMEM)
    return pl.pallas_call(
        base_kernel,
        out_shape=[
            jax.ShapeDtypeStruct(state.shape, jnp.float32),
            jax.ShapeDtypeStruct(predicted.shape, jnp.float32),
            jax.ShapeDtypeStruct((3 * v.shape[0], v.shape[1]), jnp.bfloat16),
        ],
        in_specs=[vm] * 5,
        out_specs=[vm] * 3,
        name="base",
    )(state, predicted, sums, dev, v)


def update(base_x, base_h, cross_x, cross_h, right):
    local = base_x.shape[1]
    n_x, n_h = base_x.shape[0], base_h.shape[0]
    wide = cross_x.shape[1] // STEPS
    whole = lambda n: (0, 0)
    return pl.pallas_call(
        update_kernel,
        grid=(STEPS,),
        out_shape=[
            jax.ShapeDtypeStruct(base_x.shape, jnp.float32),
            jax.ShapeDtypeStruct(base_h.shape, jnp.float32),
        ],
        in_specs=[
            pl.BlockSpec(base_x.shape, whole),
            pl.BlockSpec(base_h.shape, whole),
            pl.BlockSpec((n_x, wide), lambda n: (0, n)),
            pl.BlockSpec((n_h, wide), lambda n: (0, n)),
            pl.BlockSpec((3 * wide, local), lambda n: (n, 0)),
        ],
        out_specs=[pl.BlockSpec(base_x.shape, whole), pl.BlockSpec(base_h.shape, whole)],
        name="update",
    )(base_x, base_h, cross_x, cross_h, right)


def make(n_rows, n_mem):
    cores = 2
    n_z = n_rows // cores
    same_core = [[z * cores + c for z in range(n_z)] for c in range(cores)]
    swap = [(i, i ^ 1) for i in range(n_rows)]

    def on_device(state, predicted, perturbed, obs_variance, owners, positions):
        p = positions.shape[1]
        local = state.shape[1]
        members = local * n_mem
        row = lax.axis_index("rows")
        core = row % cores

        which = core.reshape(1).astype(jnp.int32)
        out = pick(row.reshape(1).astype(jnp.int32), owners, positions, predicted, perturbed, n_rows)
        half = out.shape[1]
        got = lax.all_to_all(
            out.reshape(n_z, cores * half, local), "rows", 0, 0, axis_index_groups=same_core, tiled=True
        )
        piece = jnp.take(got, owners // cores, axis=0, mode="clip")
        low, high = piece[:, :half], piece[:, half:]
        theirs = lax.ppermute(jnp.where(core == 0, high, low), "rows", swap)
        ours = jnp.where(core == 0, low, high)
        piece = jnp.where((owners % cores == core)[:, None, None], ours, theirs)
        here = lax.all_gather(piece, "rows", axis_index_groups=same_core)
        there = lax.ppermute(here, "rows", swap)
        inno, y, cross_x, cross_h = cross_products(which, here, there, state, predicted)
        n_gram = 6 * p // n_mem
        cross_x, cross_h = lax.psum((cross_x, cross_h), "mem")
        payload = gram_payload(which, y, state, predicted, p, n_mem)
        got = lax.all_to_all(payload, "mem", 0, 0, tiled=True)
        summed = jnp.sum(got[:, :n_gram], axis=0)
        extra = got[:, n_gram:].reshape(n_mem, -1)
        mu_all = extra[:, : 5 * p]
        n_x = -(-state.shape[0] // p) * p
        sums_all = jnp.concatenate(
            [extra[:, 5 * p : 5 * p + state.shape[0]], extra[:, 5 * p + n_x : 5 * p + n_x + predicted.shape[0]]], axis=1
        )
        here = lax.all_to_all(
            jnp.broadcast_to(summed[None], (n_mem, n_gram, p)), "mem", 0, 0, tiled=True
        ).reshape(6 * p, p)
        there = lax.ppermute(here, "rows", swap)
        dev = mu_all - jnp.sum(mu_all, axis=0, keepdims=True) / n_mem
        v = chain(
            which,
            here,
            there,
            dev,
            obs_variance,
            inno,
            float(local),
            1.0 / (members - 1),
        )
        base_x, base_h, right = base_of(state, predicted, sums_all, dev, v)
        return update(base_x, base_h, cross_x, cross_h, right)

    return on_device


def solution(mesh):
    in_specs = (P("rows", "mem"), P("rows", "mem"), P("rows", "mem"), P(), P(), P())
    out_specs = (P("rows", "mem"), P("rows", "mem"))
    inner = make(mesh.shape["rows"], mesh.shape["mem"])

    return jax.shard_map(
        inner,
        mesh=mesh,
        in_specs=in_specs,
        out_specs=out_specs,
        check_vma=False,
    )
```
